32 devices in a mesh: outer: 4 (over z), inner: 8 (over y, x, core).
Axes of the slice: x: 2, y: 2, z: 4, core: 2. Of those that a mesh axis runs over, the one named last changes fastest.
Arguments:
- queries: bfloat16 [4096, 32, 128], P(('outer', 'inner')), may hold values from -8 to 8
- key_states: bfloat16 [4096, 4, 128], P(('outer', 'inner')), may hold values from -8 to 8
- value_states: bfloat16 [4096, 4, 128], P(('outer', 'inner')), may hold values from -6 to 6
- out_grad: bfloat16 [4096, 32, 128], P(('outer', 'inner')), may hold values from -6 to 6
- bounds: int32 [3, 4096], P(None, ('outer', 'inner')), may hold values from 0 to 4095, as said below
Outputs:
- query_grad: bfloat16 [4096, 32, 128], P(('outer', 'inner'))
- key_grad: bfloat16 [4096, 4, 128], P(('outer', 'inner'))
- value_grad: bfloat16 [4096, 4, 128], P(('outer', 'inner'))
The draws below stay inside these ranges and needn't reach their ends.
Inputs may be any that keep to these rules, and one draw needn't show every extreme that they name: For each token t, bounds[0, t] is the first token of t's document (tokens of a document are consecutive), with t - 512 < bounds[0, t] <= t; in every draw some token has t - bounds[0, t] = 511. Either bounds[1, t] = bounds[2, t] = 0, or bounds[0, t] + 2 <= bounds[1, t] < bounds[2, t] <= t.
All inputs are finite; a program needn't handle non-finite values.
Results may differ from the reference program's by a relative error of at most 0.006.
Values may be sent and summed in bfloat16 or wider, within the bound.
No kernel may reach another device: no remote copies, remote signals or barrier semaphores. Data moves between devices by JAX's collectives and lax.ppermute only.
A program may use at most 64 MiB of HBM per device.

```python
import math
import jax
import jax.numpy as jnp
from jax import lax

QH = 32
KVH = 4
HD = 128
TOK_DEV = 128
SPAN = 4
TOKENS = 4096


def doc_bounds(base_key):
    longest = SPAN * TOK_DEV
    shortest = max(longest // 8, 3)
    doc_count = TOKENS // shortest + 2
    parts = jax.random.split(base_key, 6)
    short_lengths = jax.random.randint(parts[0], (doc_count,), shortest, 2 * shortest + 1)
    long_lengths = jax.random.randint(parts[1], (doc_count,), longest // 2, longest + 1)
    pick_long = jax.random.randint(parts[2], (doc_count,), 0, 4) == 0
    lengths = jnp.where(pick_long, long_lengths, short_lengths).astype(jnp.int32)
    lead_length = jax.random.randint(parts[3], (), 1, TOK_DEV).astype(jnp.int32)
    lengths = lengths.at[0].set(lead_length).at[1].set(longest)
    doc_ends = jnp.cumsum(lengths).astype(jnp.int32)
    starts = doc_ends - lengths
    prompt_share = jax.random.randint(parts[4], (doc_count,), 2, 6)
    chosen_share = jax.random.randint(parts[5], (doc_count,), 2, 7)
    prompt = jnp.minimum(jnp.maximum(lengths * prompt_share // 8, 2), lengths)
    chosen = (lengths - prompt) * chosen_share // 8
    positions = jnp.arange(TOKENS, dtype=jnp.int32)
    doc_index = jnp.searchsorted(doc_ends, positions, side='right').astype(jnp.int32)
    doc_start = starts[doc_index]
    skip_low = doc_start + prompt[doc_index]
    skip_high = skip_low + chosen[doc_index]
    in_skip = (positions >= skip_high) & (skip_high > skip_low)
    low_edge = jnp.where(in_skip, skip_low, 0)
    high_edge = jnp.where(in_skip, skip_high, 0)
    frame = jnp.stack([doc_start, low_edge, high_edge]).astype(jnp.int32)
    return frame


def draw_bounds(key, part):
    frame = doc_bounds(jax.random.fold_in(key, 7))
    return frame


def draw_queries(key, part):
    values = jnp.clip(jax.random.normal(jax.random.fold_in(key, 21), (TOKENS, QH, HD), jnp.float32), -6.0, 6.0)
    return values.astype(jnp.bfloat16)


def draw_key_states(key, part):
    values = jnp.clip(jax.random.normal(jax.random.fold_in(key, 23), (TOKENS, KVH, HD), jnp.float32), -6.0, 6.0)
    return values.astype(jnp.bfloat16)


def block_levels(key, extent, pieces, least, largest):
    gain, own = 1.0, jax.random.fold_in(key, 6)
    for position, shards_of in pieces:
        heights = jnp.exp(jax.random.uniform(jax.random.fold_in(own, position), (shards_of,), jnp.float32, least / len(pieces), largest / len(pieces)))
        gain = gain * jnp.repeat(heights, extent[position] // shards_of).reshape([-1 if axis == position else 1 for axis in range(len(extent))])
    return gain


def gaussian(own_key, dims, scale, most, pieces=(), kind=jnp.bfloat16):
    entries = scale * jax.random.normal(own_key, dims, jnp.float32)
    if pieces:
        entries = entries * block_levels(own_key, dims, pieces, -0.22, 0.18)
    return jnp.clip(entries, -most, most).astype(kind)


def setup_inputs(seed: int = 0) -> dict:
    key_list = jax.random.split(jax.random.key(seed), 6)
    queries = draw_queries(jax.random.fold_in(key_list[5], 71), 0)
    key_states = draw_key_states(jax.random.fold_in(key_list[5], 71), 0)
    value_states = gaussian(key_list[2], (TOKENS, KVH, HD), 1.0, 6.0, ((0, 32),))
    out_grad = gaussian(key_list[3], (TOKENS, QH, HD), 1.0, 6.0, ((0, 32),))
    bounds = draw_bounds(jax.random.fold_in(key_list[5], 71), 0)
    return dict(queries=queries, key_states=key_states, value_states=value_states, out_grad=out_grad, bounds=bounds)


def visible(query_pos, key_pos, bounds):
    doc_start = bounds[0][:, None]
    skip_low = bounds[1][:, None]
    skip_high = bounds[2][:, None]
    key_row = key_pos[None, :]
    return (key_row >= doc_start) & (key_row <= query_pos[:, None]) & ((key_row < skip_low) | (key_row >= skip_high))


def reference(queries, key_states, value_states, out_grad, bounds):
    group_size = QH // KVH
    reach_rows = SPAN * TOK_DEV
    block_rows = math.gcd(512, TOKENS)
    score_scale = HD ** -0.5
    padded_keys = jnp.pad(key_states, ((reach_rows, 0), (0, 0), (0, 0)))
    padded_values = jnp.pad(value_states, ((reach_rows, 0), (0, 0), (0, 0)))
    query_four = queries.reshape(TOKENS, KVH, group_size, HD)
    grad_four = out_grad.reshape(TOKENS, KVH, group_size, HD)

    def scan_step(carried, block_index):
        key_sums, value_sums = carried
        first_row = block_index * block_rows
        query_block = lax.dynamic_slice_in_dim(query_four, first_row, block_rows, 0).astype(jnp.float32)
        grad_block = lax.dynamic_slice_in_dim(grad_four, first_row, block_rows, 0).astype(jnp.float32)
        key_block = lax.dynamic_slice_in_dim(padded_keys, first_row, block_rows + reach_rows, 0).astype(jnp.float32)
        value_block = lax.dynamic_slice_in_dim(padded_values, first_row, block_rows + reach_rows, 0).astype(jnp.float32)
        bound_block = lax.dynamic_slice_in_dim(bounds, first_row, block_rows, 1)
        query_pos = first_row + jnp.arange(block_rows, dtype=jnp.int32)
        key_pos = first_row - reach_rows + jnp.arange(block_rows + reach_rows, dtype=jnp.int32)
        seen_mask = visible(query_pos, key_pos, bound_block)
        scores = jnp.einsum("tkgd,skd->kgts", query_block, key_block) * score_scale
        grad_weights = jnp.einsum("tkgd,skd->kgts", grad_block, value_block)
        row_max = jnp.max(jnp.where(seen_mask, scores, -jnp.inf), axis=-1, keepdims=True)
        raw_weights = jnp.exp(jnp.where(seen_mask, scores - row_max, -jnp.inf))
        row_total = jnp.sum(raw_weights, axis=-1, keepdims=True)
        log_total = row_max + jnp.log(row_total)
        row_delta = jnp.sum(raw_weights * grad_weights, axis=-1, keepdims=True) / row_total
        prob = jnp.exp(jnp.where(seen_mask, scores - log_total, -jnp.inf))
        weights = lax.optimization_barrier(prob.astype(jnp.bfloat16)).astype(jnp.float32)
        dscore = lax.optimization_barrier((score_scale * prob * (grad_weights - row_delta)).astype(jnp.bfloat16)).astype(jnp.float32)
        query_part = jnp.einsum("kgts,skd->tkgd", dscore, key_block).reshape(block_rows, QH, HD).astype(jnp.bfloat16)
        key_part = jnp.einsum("kgts,tkgd->skd", dscore, query_block)
        value_part = jnp.einsum("kgts,tkgd->skd", weights, grad_block)
        key_sums = lax.dynamic_update_slice_in_dim(key_sums, lax.dynamic_slice_in_dim(key_sums, first_row, block_rows + reach_rows, 0) + key_part, first_row, 0)
        value_sums = lax.dynamic_update_slice_in_dim(value_sums, lax.dynamic_slice_in_dim(value_sums, first_row, block_rows + reach_rows, 0) + value_part, first_row, 0)
        return (key_sums, value_sums), query_part

    start_sums = jnp.zeros((TOKENS + reach_rows, KVH, HD), jnp.float32)
    (key_sums, value_sums), query_parts = lax.scan(scan_step, (start_sums, start_sums), jnp.arange(TOKENS // block_rows, dtype=jnp.int32))
    query_grad = query_parts.reshape(TOKENS, QH, HD)
    key_grad = key_sums[reach_rows:].astype(jnp.bfloat16)
    value_grad = value_sums[reach_rows:].astype(jnp.bfloat16)
    return (query_grad, key_grad, value_grad)
```

```python
import math

import jax
import jax.numpy as jnp
from jax import lax
from jax.experimental import pallas as pl
from jax.experimental.pallas import tpu as pltpu
from jax.sharding import PartitionSpec as P

AXES = ("outer", "inner")
SPAN = 4
HIDDEN = -1e30
VMEM = pl.BlockSpec(memory_space=pltpu.VMEM)
NT = (((1,), (1,)), ((), ()))
NN = (((1,), (0,)), ((), ()))


def rotated(shard, by):
    peers = lax.axis_size(AXES)
    return lax.ppermute(shard, AXES, [(i, (i + by) % peers) for i in range(peers)])


def swapped(shard):
    peers = lax.axis_size(AXES)
    return lax.ppermute(shard, AXES, [(i, i ^ 1) for i in range(peers)])


def dot(a, b, dims):
    return lax.dot_general(a, b, dims, preferred_element_type=jnp.float32)


def call(body, outs, args, scratch=(), cost=None, mib=24):
    return pl.pallas_call(
        body,
        out_shape=outs,
        in_specs=[VMEM] * len(args),
        out_specs=jax.tree.map(lambda _: VMEM, outs),
        scratch_shapes=list(scratch),
        compiler_params=pltpu.CompilerParams(vmem_limit_bytes=mib << 20),
        cost_estimate=pl.CostEstimate(flops=cost or 0, bytes_accessed=1 << 20, transcendentals=0),
    )(*args)


def pack_body(k_ref, v_ref, kv_ref):
    heads = k_ref.shape[1]
    for c in range(heads):
        kv_ref[c] = k_ref[:, c, :]
        kv_ref[heads + c] = v_ref[:, c, :]


def prepare_body(q_ref, g_ref, kv_ref, edges_ref, qr_ref, gr_ref, bias_ref, s_ref, w_ref):
    rows, heads, depth = q_ref.shape
    kv_heads = kv_ref.shape[0] // 2
    group = heads // kv_heads
    lanes = rows * group
    for c in range(kv_heads):
        own = slice(c * group, (c + 1) * group)
        qr_ref[c] = q_ref[:, own, :].astype(jnp.float32).reshape(lanes, depth).astype(jnp.bfloat16)
        gr_ref[c] = g_ref[:, own, :].astype(jnp.float32).reshape(lanes, depth).astype(jnp.bfloat16)
        s_ref[c] = dot(kv_ref[c], qr_ref[c], NT)
        w_ref[c] = dot(kv_ref[kv_heads + c], gr_ref[c], NT)
    local = lax.broadcasted_iota(jnp.int32, (rows, lanes), 0)
    token = lax.broadcasted_iota(jnp.int32, (rows, lanes), 1) // group
    start, low, high = edges_ref[0:1, :], edges_ref[1:2, :], edges_ref[2:3, :]
    for o in range(SPAN):
        if o == 0:
            key = jnp.where(local <= token, local, local - SPAN * rows)
        else:
            key = local - o * rows
        seen = (key >= start) & ((key < low) | (key >= high))
        bias_ref[o] = jnp.where(seen, 0.0, HIDDEN)


def main_body(*refs):
    kv_refs, (qr_ref, gr_ref, bias_ref, s_ref, w_ref), outs = refs[:SPAN], refs[SPAN : SPAN + 5], refs[SPAN + 5 :]
    part_refs, (ds_ref, p_ref, pm_ref) = outs[:SPAN], outs[SPAN:]
    kv_heads, lanes, depth = qr_ref.shape
    rows = s_ref.shape[1]
    scale = depth ** -0.5
    width = 256
    group = lanes // rows
    for c in range(kv_heads):
        for n in range(lanes // width):
            cols = slice(n * width, (n + 1) * width)
            q = qr_ref[c, cols, :]
            g = gr_ref[c, cols, :]
            local = lax.broadcasted_iota(jnp.int32, (rows, width), 0)
            token = lax.broadcasted_iota(jnp.int32, (rows, width), 1) // group + n * (width // group)
            inside = local <= token
            scores, weighs = [], []
            for o in range(SPAN):
                kv_ref = kv_refs[(o - 1) % SPAN]
                s = dot(kv_ref[c], q, NT)
                w = dot(kv_ref[kv_heads + c], g, NT)
                if o == 0:
                    s = jnp.where(inside, s_ref[c, :, cols], s)
                    w = jnp.where(inside, w_ref[c, :, cols], w)
                scores.append(s + bias_ref[o, :, cols])
                weighs.append(w)
            top = jnp.max(jnp.maximum(jnp.maximum(scores[0], scores[1]), jnp.maximum(scores[2], scores[3])), axis=0, keepdims=True)
            raw = [jnp.exp2((s - top) * (scale * math.log2(math.e))) for s in scores]
            total = jnp.sum(sum(raw), axis=0, keepdims=True)
            inverse = 1.0 / total
            delta = jnp.sum(sum(e * w for e, w in zip(raw, weighs)), axis=0, keepdims=True) * inverse
            for o in range(SPAN):
                prob = raw[o] * inverse
                dscore = (prob * scale) * (weighs[o] - delta)
                if o == 0:
                    p_ref[c, :, cols] = jnp.where(inside, prob, 0.0).astype(jnp.bfloat16)
                    ds_ref[c, SPAN * rows :, cols] = jnp.where(inside, dscore, 0.0).astype(jnp.bfloat16)
                    prob = jnp.where(inside, 0.0, prob)
                    dscore = jnp.where(inside, 0.0, dscore)
                at = slice(((o - 1) % SPAN) * rows, ((o - 1) % SPAN + 1) * rows)
                pm_ref[at, cols] = prob.astype(jnp.bfloat16)
                ds_ref[c, at, cols] = dscore.astype(jnp.bfloat16)
        dk = dot(ds_ref[c, : SPAN * rows, :], qr_ref[c], NN).astype(jnp.bfloat16)
        dv = dot(pm_ref[...], gr_ref[c], NN).astype(jnp.bfloat16)
        for o in range(SPAN):
            part_refs[o][c] = dk[o * rows : (o + 1) * rows]
            part_refs[o][kv_heads + c] = dv[o * rows : (o + 1) * rows]


def query_body(*refs):
    kv_refs, (ds_ref, p_ref, qr_ref, gr_ref), (dq_ref, own_ref, turned_ref) = refs[: SPAN + 1], refs[SPAN + 1 : SPAN + 5], refs[SPAN + 5 :]
    kv_heads, lanes, depth = qr_ref.shape
    rows = p_ref.shape[1]
    group = lanes // rows
    for c in range(kv_heads):
        own_ref[c] = dot(ds_ref[c, SPAN * rows :, :], qr_ref[c], NN)
        own_ref[kv_heads + c] = dot(p_ref[c], gr_ref[c], NN)
        for o in range(SPAN + 1):
            turned_ref[:, o * rows : (o + 1) * rows] = kv_refs[o][c].astype(jnp.float32).T.astype(jnp.bfloat16)
        dq = dot(turned_ref[...], ds_ref[c], NN).T
        dq_ref[:, c * group : (c + 1) * group, :] = dq.reshape(rows, group, depth).astype(jnp.bfloat16)


def finish_body(own_ref, near_ref, far_ref, dk_ref, dv_ref):
    kv_heads = own_ref.shape[0] // 2
    for c in range(kv_heads):
        for out_ref, at in ((dk_ref, c), (dv_ref, kv_heads + c)):
            total = own_ref[at] + near_ref[at].astype(jnp.float32) + far_ref[at].astype(jnp.float32)
            out_ref[:, c, :] = total.astype(jnp.bfloat16)


def per_device(queries, key_states, value_states, out_grad, bounds):
    rows, heads, depth = queries.shape
    kv_heads = key_states.shape[1]
    group = heads // kv_heads
    lanes = rows * group
    bf, f32 = jnp.bfloat16, jnp.float32
    shape = jax.ShapeDtypeStruct
    my_index = lax.axis_index(AXES)
    odd = lax.rem(my_index, 2) == 1
    product = 2 * kv_heads * rows * lanes * depth

    own = call(pack_body, shape((2 * kv_heads, rows, depth), bf), (key_states, value_states))
    far = rotated(own, 4)
    near = rotated(own, 2)
    edges = jnp.repeat(bounds - my_index * rows, group, axis=1)
    qr, gr, bias, s_own, w_own = call(
        prepare_body,
        (
            shape((kv_heads, lanes, depth), bf),
            shape((kv_heads, lanes, depth), bf),
            shape((SPAN, rows, lanes), f32),
            shape((kv_heads, rows, lanes), f32),
            shape((kv_heads, rows, lanes), f32),
        ),
        (queries, out_grad, own, edges),
        cost=2 * product,
    )
    one = swapped(jnp.where(odd, near, own))
    three = swapped(jnp.where(odd, far, near))
    block = shape((2 * kv_heads, rows, depth), bf)
    g1, g2, g3, g4, dscore, p_own = call(
        main_body,
        (block,) * SPAN + (shape((kv_heads, (SPAN + 1) * rows, lanes), bf), shape((kv_heads, rows, lanes), bf)),
        (one, near, three, far, qr, gr, bias, s_own, w_own),
        scratch=(pltpu.VMEM((SPAN * rows, lanes), bf),),
        cost=16 * product,
        mib=40,
    )
    b1 = swapped(g1)
    b3 = swapped(g3)
    dq, own_sum = call(
        query_body,
        (shape((rows, heads, depth), bf), shape((2 * kv_heads, rows, depth), f32)),
        (one, near, three, far, own, dscore, p_own, qr, gr),
        scratch=(pltpu.VMEM((depth, (SPAN + 1) * rows), bf),),
        cost=7 * product,
        mib=32,
    )
    b1, b3, g2, g4 = (x.astype(f32) for x in (b1, b3, g2, g4))
    zero = jnp.zeros_like(b1)
    to_near = (g2 + jnp.where(odd, b1, b3)).astype(bf)
    to_far = (g4 + jnp.where(odd, b3, zero)).astype(bf)
    from_far = rotated(to_far, -4)
    from_near = rotated(to_near, -2)
    own_sum = own_sum + jnp.where(odd, zero, b1)
    dk, dv = call(finish_body, (shape(key_states.shape, bf), shape(value_states.shape, bf)), (own_sum, from_near, from_far))
    return dq, dk, dv


def solution(mesh):
    rows = P(AXES, None, None)
    return jax.shard_map(
        per_device,
        mesh=mesh,
        in_specs=(rows, rows, rows, rows, P(None, AXES)),
        out_specs=(rows, rows, rows),
        check_vma=False,
    )
```

```python
import functools
import math

import jax
import jax.numpy as jnp
from jax import lax
from jax.experimental import pallas as pl
from jax.experimental.pallas import tpu as pltpu
from jax.sharding import PartitionSpec as P

AXES = ("outer", "inner")
SPAN = 4
HIDDEN = -1e30
VMEM = pl.BlockSpec(memory_space=pltpu.VMEM)
SMEM = pl.BlockSpec(memory_space=pltpu.SMEM)
HBM = pl.BlockSpec(memory_space=pltpu.HBM)
NT = (((1,), (1,)), ((), ()))
NN = (((1,), (0,)), ((), ()))
BF = jnp.bfloat16
F32 = jnp.float32
TILE = 32
WIDTH = 256
CHUNKS = 2


def rotated(shard, by):
    peers = lax.axis_size(AXES)
    return lax.ppermute(shard, AXES, [(i, (i + by) % peers) for i in range(peers)])


def swapped(shard):
    peers = lax.axis_size(AXES)
    return lax.ppermute(shard, AXES, [(i, i ^ 1) for i in range(peers)])


def dot(a, b, dims):
    return lax.dot_general(a, b, dims, preferred_element_type=F32)


def call(body, outs, args, specs=None, scratch=(), flops=0, mib=16, name=None, flags=None):
    return pl.pallas_call(
        body,
        out_shape=outs,
        in_specs=specs or [VMEM] * len(args),
        out_specs=jax.tree.map(lambda _: VMEM, outs),
        scratch_shapes=list(scratch),
        compiler_params=pltpu.CompilerParams(vmem_limit_bytes=mib << 20, flags=flags),
        cost_estimate=pl.CostEstimate(flops=flops, bytes_accessed=1 << 20, transcendentals=0),
        name=name,
    )(*args)


def pack_body(k_ref, v_ref, *refs):
    kv_refs, wide_ref = refs[:-1], refs[-1]
    part, rows, _ = kv_refs[0].shape
    part //= 2
    heads = part * CHUNKS
    for half, ref in enumerate((k_ref, v_ref)):
        wide_ref[half] = ref[...].astype(F32)
        for c in range(heads):
            kv_refs[c // part][half * part + c % part] = wide_ref[half, pl.ds(c, rows, stride=heads), :].astype(BF)


def prepare_body(me_ref, q_ref, g_ref, bounds_ref, *refs):
    kv_refs, (qr_ref, gr_ref, bias_ref, s_ref, w_ref) = refs[:CHUNKS], refs[CHUNKS:]
    rows, heads, depth = q_ref.shape
    kv_heads = qr_ref.shape[0]
    part = kv_heads // CHUNKS
    group = heads // kv_heads
    lanes = rows * group
    for c in range(kv_heads):
        own = slice(c * group, (c + 1) * group)
        qr_ref[c] = q_ref[:, own, :].astype(F32).reshape(lanes, depth).astype(BF)
        gr_ref[c] = g_ref[:, own, :].astype(F32).reshape(lanes, depth).astype(BF)
        s_ref[c] = dot(kv_refs[c // part][c % part], qr_ref[c], NT)
        w_ref[c] = dot(kv_refs[c // part][part + c % part], gr_ref[c], NT)
    local = lax.broadcasted_iota(jnp.int32, (rows, rows), 0)
    token = lax.broadcasted_iota(jnp.int32, (rows, rows), 1)
    wide_token = lax.broadcasted_iota(jnp.int32, (rows, lanes), 0)
    wide_lane = lax.broadcasted_iota(jnp.int32, (rows, lanes), 1)
    widen = (wide_lane // group == wide_token).astype(BF)
    me = me_ref[0]
    odd = lax.rem(me, 2)
    start = bounds_ref[0:1, :] - me * rows
    low = bounds_ref[1:2, :] - me * rows
    high = bounds_ref[2:3, :] - me * rows
    x_offset = 1 + 2 * odd
    for at, offset in enumerate((SPAN, 2, x_offset, SPAN - x_offset)):
        key = local - offset * rows
        if at == 0:
            key = jnp.where(local <= token, local, key)
        seen = (key >= start) & ((key < low) | (key >= high))
        bias_ref[at * rows : (at + 1) * rows, :] = dot(jnp.where(seen, 0.0, HIDDEN).astype(BF), widen, NN)


def main_body(first, *refs):
    me_ref, refs = refs[0], refs[1:]
    kv_refs = refs[:SPAN]
    qr_ref, gr_ref, bias_ref, s_ref, w_ref = refs[SPAN : SPAN + 5]
    part_refs = refs[SPAN + 5 : 2 * SPAN + 5]
    ds_ref, p_ref = refs[2 * SPAN + 5 : 2 * SPAN + 7]
    k_all, v_all, s_all, w_all, p_all, stat = refs[2 * SPAN + 7 :]
    _, lanes, depth = qr_ref.shape
    kv_heads = kv_refs[0].shape[0] // 2
    rows = s_ref.shape[1]
    far = SPAN * rows
    scale = depth ** -0.5
    rate = scale * math.log2(math.e)
    group = lanes // rows
    chunks = lanes // WIDTH
    steps = [(c, n) for c in range(kv_heads) for n in range(chunks)]
    fold = lambda x: x.reshape(TILE // 8, 8, WIDTH)
    region = pl.when(me_ref[0] >= 0)
    tiles = [slice(r, r + TILE) for r in range(0, far, TILE)]

    def inside(r, n):
        local = lax.broadcasted_iota(jnp.int32, (TILE, WIDTH), 0) + r
        token = lax.broadcasted_iota(jnp.int32, (TILE, WIDTH), 1) // group + n * (WIDTH // group)
        return local <= token

    def gather(c):
        for o in range(SPAN):
            k_all[c % 2, o * rows : (o + 1) * rows, :] = kv_refs[o][c]
            v_all[c % 2, o * rows : (o + 1) * rows, :] = kv_refs[o][kv_heads + c]

    def score(t):
        c, n = steps[t]
        slot, cols = t % 2, slice(n * WIDTH, (n + 1) * WIDTH)
        s = dot(k_all[c % 2], qr_ref[first + c, cols, :], NT)
        top = jnp.full((8, WIDTH), HIDDEN, F32)
        for at in tiles:
            s_tile = s[at]
            if at.start < rows:
                s_tile = jnp.where(inside(at.start, n), s_ref[first + c, at, cols], s_tile)
            s_tile = s_tile + bias_ref[at, cols]
            s_all[slot, at, :] = s_tile
            top = jnp.maximum(top, jnp.max(fold(s_tile), axis=0))
        stat[slot, 0] = jnp.broadcast_to(jnp.max(top, axis=0, keepdims=True), (8, WIDTH))

    def weigh(t):
        c, n = steps[t]
        slot, cols = t % 2, slice(n * WIDTH, (n + 1) * WIDTH)
        w = dot(v_all[c % 2], gr_ref[first + c, cols, :], NT)
        for at in tiles:
            w_tile = w[at]
            if at.start < rows:
                w_tile = jnp.where(inside(at.start, n), w_ref[first + c, at, cols], w_tile)
            w_all[slot, at, :] = w_tile

    def spread(t):
        slot = t % 2
        top = stat[slot, 0, 0:1, :]
        total = jnp.zeros((8, WIDTH), F32)
        delta = jnp.zeros((8, WIDTH), F32)
        for at in tiles:
            e = jnp.exp2((s_all[slot, at, :] - top) * rate)
            s_all[slot, at, :] = e
            total = total + jnp.sum(fold(e), axis=0)
            delta = delta + jnp.sum(fold(e * w_all[slot, at, :]), axis=0)
        inverse = 1.0 / jnp.sum(total, axis=0, keepdims=True)
        delta = jnp.sum(delta, axis=0, keepdims=True) * inverse
        stat[slot, 1] = jnp.broadcast_to(inverse, (8, WIDTH))
        stat[slot, 2] = jnp.broadcast_to(delta, (8, WIDTH))

    def settle(t):
        c, n = steps[t]
        slot, cols = t % 2, slice(n * WIDTH, (n + 1) * WIDTH)
        inverse, delta = stat[slot, 1, 0:1, :], stat[slot, 2, 0:1, :]
        for at in tiles:
            prob = s_all[slot, at, :] * inverse
            dscore = ((prob * scale) * (w_all[slot, at, :] - delta)).astype(BF)
            prob = prob.astype(BF)
            if at.start < rows:
                here = inside(at.start, n)
                zero = jnp.zeros_like(prob)
                p_ref[c, at, cols] = jnp.where(here, prob, zero)
                ds_ref[c, far + at.start : far + at.stop, cols] = jnp.where(here, dscore, zero)
                prob = jnp.where(here, zero, prob)
                dscore = jnp.where(here, zero, dscore)
            p_all[c % 2, at, cols] = prob
            ds_ref[c, at, cols] = dscore

    def key_grad(c):
        dk = dot(ds_ref[c, :far, :], qr_ref[first + c], NN).astype(BF)
        for o in range(SPAN):
            part_refs[o][c] = dk[o * rows : (o + 1) * rows]

    def value_grad(c):
        dv = dot(p_all[c % 2], gr_ref[first + c], NN).astype(BF)
        for o in range(SPAN):
            part_refs[o][kv_heads + c] = dv[o * rows : (o + 1) * rows]

    @region
    def _():
        gather(0)

    @region
    def _():
        score(0)
        weigh(0)

    for t, (c, n) in enumerate(steps):
        following = t + 1 < len(steps)

        @region
        def _():
            spread(t)
            if n == chunks - 1 and following:
                gather(c + 1)
            if n == 0 and c:
                key_grad(c - 1)
            if following and n < chunks - 1:
                score(t + 1)

        @region
        def _():
            settle(t)
            if n == 0 and c:
                value_grad(c - 1)
            if following:
                if n == chunks - 1:
                    score(t + 1)
                weigh(t + 1)

    @region
    def _():
        key_grad(kv_heads - 1)
        value_grad(kv_heads - 1)


def query_body(*refs):
    per = SPAN + 3
    groups = [refs[per * i : per * (i + 1)] for i in range(CHUNKS)]
    qr_ref, gr_ref, dq_ref, own_ref, turned_ref = refs[per * CHUNKS :]
    kv_heads, lanes, depth = qr_ref.shape
    part = kv_heads // CHUNKS
    rows = dq_ref.shape[0]
    group = lanes // rows
    for c in range(kv_heads):
        *kv_refs, ds_ref, p_ref = groups[c // part]
        at = c % part
        own_ref[c] = dot(ds_ref[at, SPAN * rows :, :], qr_ref[c], NN)
        own_ref[kv_heads + c] = dot(p_ref[at], gr_ref[c], NN)
        for o in range(SPAN + 1):
            turned_ref[:, o * rows : (o + 1) * rows] = kv_refs[o][at].astype(F32).T.astype(BF)
        dq = dot(turned_ref[...], ds_ref[at], NN).T
        dq_ref[:, c * group : (c + 1) * group, :] = dq.reshape(rows, group, depth).astype(BF)


def finish_body(own_ref, *refs):
    groups, (dk_ref, dv_ref, wide_ref) = [refs[3 * i : 3 * i + 3] for i in range(CHUNKS)], refs[3 * CHUNKS :]
    kv_heads, rows, _ = own_ref.shape
    kv_heads //= 2
    part = kv_heads // CHUNKS
    for half, out_ref in enumerate((dk_ref, dv_ref)):
        for c in range(kv_heads):
            total = own_ref[half * kv_heads + c]
            for ref in groups[c // part]:
                total = total + ref[half * part + c % part].astype(F32)
            wide_ref[half, pl.ds(c, rows, stride=kv_heads), :] = total
        out_ref[...] = wide_ref[half].astype(BF)


def per_device(queries, key_states, value_states, out_grad, bounds):
    rows, heads, depth = queries.shape
    kv_heads = key_states.shape[1]
    part = kv_heads // CHUNKS
    group = heads // kv_heads
    lanes = rows * group
    shape = jax.ShapeDtypeStruct
    my_index = lax.axis_index(AXES)
    odd = lax.rem(my_index, 2) == 1
    product = 2 * kv_heads * rows * lanes * depth
    block = shape((2 * part, rows, depth), BF)
    zero = jnp.zeros(block.shape, BF)

    flat = shape((rows * kv_heads, depth), BF)
    owns = call(
        pack_body,
        (block,) * CHUNKS,
        (key_states.reshape(flat.shape), value_states.reshape(flat.shape)),
        scratch=(pltpu.VMEM((2, *flat.shape), F32),),
        name="pack",
    )
    sent = [(rotated(own, 4), rotated(own, 2)) for own in owns]
    ready = call(
        prepare_body,
        (
            shape((kv_heads, lanes, depth), BF),
            shape((kv_heads, lanes, depth), BF),
            shape((SPAN * rows, lanes), F32),
            shape((kv_heads, rows, lanes), F32),
            shape((kv_heads, rows, lanes), F32),
        ),
        (my_index.reshape(1), queries, out_grad, bounds, *owns),
        specs=[SMEM] + [VMEM] * (3 + CHUNKS),
        flops=2 * product,
        name="prepare",
    )
    qr, gr = ready[:2]
    blocks, scores, backs, rests = [], [], [], []
    parts = back = None
    for i in range(CHUNKS):
        (far, near), ready = lax.optimization_barrier((sent[i], ready))
        x, y = swapped(near), swapped(jnp.where(odd, far, owns[i]))
        if back is not None:
            (x, y), back = lax.optimization_barrier(((x, y), back))
            backs.append((rotated(back[0], -4), rotated(back[1], -2)))
        *parts, dscore, prob = call(
            functools.partial(main_body, i * part),
            (block,) * SPAN
            + (
                shape((part, (SPAN + 1) * rows, lanes), BF),
                shape((part, rows, lanes), BF),
            ),
            (my_index.reshape(1), far, near, x, y, *ready),
            specs=[SMEM] + [VMEM] * 9,
            scratch=(
                pltpu.VMEM((2, SPAN * rows, depth), BF),
                pltpu.VMEM((2, SPAN * rows, depth), BF),
                pltpu.VMEM((2, SPAN * rows, WIDTH), F32),
                pltpu.VMEM((2, SPAN * rows, WIDTH), F32),
                pltpu.VMEM((2, SPAN * rows, lanes), BF),
                pltpu.VMEM((2, 3, 8, WIDTH), F32),
            ),
            flops=16 * product // CHUNKS,
            mib=18,
            name=f"main{i}",
        )
        blocks.append((far, near, x, y, owns[i]))
        scores.append((dscore, prob))
        if i + 1 < CHUNKS:
            sent[i + 1], parts = lax.optimization_barrier((sent[i + 1], parts))
        g_far, g_near, g_x, g_y = parts
        back_x, back_y = swapped(g_x), swapped(g_y)
        back = (
            (g_far.astype(F32) + jnp.where(odd, back_y, zero).astype(F32)).astype(BF),
            (g_near.astype(F32) + back_x.astype(F32)).astype(BF),
        )
        rests.append(jnp.where(odd, zero, back_y))
    back, scores[-1] = lax.optimization_barrier((back, scores[-1]))
    backs.append((rotated(back[0], -4), rotated(back[1], -2)))
    inputs = []
    for block_refs, score in zip(blocks, scores):
        inputs += [*block_refs, *score]
    dq, own_sum = call(
        query_body,
        (shape((rows, heads, depth), BF), shape((2 * kv_heads, rows, depth), F32)),
        (*inputs, qr, gr),
        scratch=(pltpu.VMEM((depth, (SPAN + 1) * rows), BF),),
        flops=7 * product,
        name="query",
    )
    inputs = []
    for rest, got in zip(rests, backs):
        inputs += [rest, *got]
    dk, dv = call(
        finish_body,
        (flat, flat),
        (own_sum, *inputs),
        scratch=(pltpu.VMEM((2, *flat.shape), F32),),
        name="finish",
    )
    return dq, dk.reshape(key_states.shape), dv.reshape(value_states.shape)


def solution(mesh):
    rows = P(AXES, None, None)
    return jax.shard_map(
        per_device,
        mesh=mesh,
        in_specs=(rows, rows, rows, rows, P(None, AXES)),
        out_specs=(rows, rows, rows),
        check_vma=False,
    )
```

```python
import functools
import math

import jax
import jax.numpy as jnp
from jax import lax
from jax.experimental import pallas as pl
from jax.experimental.pallas import tpu as pltpu
from jax.sharding import PartitionSpec as P


AXES = ("outer", "inner")
SPAN = 4
HIDDEN = -1e30
VMEM = pl.BlockSpec(memory_space=pltpu.VMEM)
SMEM = pl.BlockSpec(memory_space=pltpu.SMEM)
HBM = pl.BlockSpec(memory_space=pltpu.HBM)
NT = (((1,), (1,)), ((), ()))
NN = (((1,), (0,)), ((), ()))
BF = jnp.bfloat16
F32 = jnp.float32
TILE = 32
WIDTH = 256
CHUNKS = 2


def rotated(shard, by):
    peers = lax.axis_size(AXES)
    return lax.ppermute(shard, AXES, [(i, (i + by) % peers) for i in range(peers)])


def rotated_pair(shards, way):
    far = rotated(shards[0], way * SPAN)
    near = rotated(shards[1], way * SPAN // 2)
    return far, near


def swapped(shard):
    peers = lax.axis_size(AXES)
    return lax.ppermute(shard, AXES, [(i, i ^ 1) for i in range(peers)])


def dot(a, b, dims):
    return lax.dot_general(a, b, dims, preferred_element_type=F32)


def in_hbm(x):
    return pltpu.with_memory_space_constraint(x, pltpu.HBM)


def call(body, outs, args, specs=None, scratch=(), flops=0, mib=16):
    return pl.pallas_call(
        body,
        out_shape=outs,
        in_specs=specs or [VMEM] * len(args),
        out_specs=jax.tree.map(lambda _: VMEM, outs),
        scratch_shapes=list(scratch),
        compiler_params=pltpu.CompilerParams(vmem_limit_bytes=mib << 20),
        cost_estimate=pl.CostEstimate(flops=flops, bytes_accessed=1 << 20, transcendentals=0),
    )(*args)


def fetch(sources, targets, sems):
    copies = [pltpu.make_async_copy(a, b, sems.at[i]) for i, (a, b) in enumerate(zip(sources, targets))]
    for copy in copies:
        copy.start()
    return copies


def pack_body(k_hbm, v_hbm, *refs):
    kv_refs, (raw_ref, wide_ref, sems) = refs[:-3], refs[-3:]
    part, rows, _ = kv_refs[0].shape
    part //= 2
    heads = part * CHUNKS
    copies = fetch((k_hbm, v_hbm), (raw_ref.at[0], raw_ref.at[1]), sems)
    for half in range(2):
        copies[half].wait()
        wide_ref[half] = raw_ref[half].astype(F32)
        for c in range(heads):
            kv_refs[c // part][half * part + c % part] = wide_ref[half, pl.ds(c, rows, stride=heads), :].astype(BF)


def prepare_body(me_ref, q_hbm, g_hbm, bounds_ref, *refs):
    kv_refs, (qr_ref, gr_ref, bias_ref, s_ref, w_ref, q_ref, g_ref, sems) = refs[:CHUNKS], refs[CHUNKS:]
    copies = fetch((q_hbm, g_hbm), (q_ref, g_ref), sems)
    rows, heads, depth = q_ref.shape
    kv_heads = qr_ref.shape[0]
    part = kv_heads // CHUNKS
    group = heads // kv_heads
    lanes = rows * group
    local = lax.broadcasted_iota(jnp.int32, (rows, rows), 0)
    token = lax.broadcasted_iota(jnp.int32, (rows, rows), 1)
    wide_token = lax.broadcasted_iota(jnp.int32, (rows, lanes), 0)
    wide_lane = lax.broadcasted_iota(jnp.int32, (rows, lanes), 1)
    widen = (wide_lane // group == wide_token).astype(BF)
    me = me_ref[0]
    odd = lax.rem(me, 2)
    start = bounds_ref[0:1, :] - me * rows
    low = bounds_ref[1:2, :] - me * rows
    high = bounds_ref[2:3, :] - me * rows
    x_offset = 1 + 2 * odd
    for at, offset in enumerate((SPAN, 2, x_offset, SPAN - x_offset)):
        key = local - offset * rows
        if at == 0:
            key = jnp.where(local <= token, local, key)
        seen = (key >= start) & ((key < low) | (key >= high))
        bias_ref[at * rows : (at + 1) * rows, :] = dot(jnp.where(seen, 0.0, HIDDEN).astype(BF), widen, NN)
    for copy in copies:
        copy.wait()
    for c in range(kv_heads):
        own = slice(c * group, (c + 1) * group)
        qr_ref[c] = q_ref[:, own, :].astype(F32).reshape(lanes, depth).astype(BF)
        gr_ref[c] = g_ref[:, own, :].astype(F32).reshape(lanes, depth).astype(BF)
        s_ref[c] = dot(kv_refs[c // part][c % part], qr_ref[c], NT)
        w_ref[c] = dot(kv_refs[c // part][part + c % part], gr_ref[c], NT)


def lanes_of(far_ref, near_ref, pair_ref):
    half = pair_ref.shape[0] // 2
    return far_ref, near_ref, pair_ref.at[:half], pair_ref.at[half:]


def main_body(first, *refs):
    me_ref, refs = refs[0], refs[1:]
    kv_refs = lanes_of(*refs[:3])
    qr_ref, gr_ref, bias_ref, s_ref, w_ref = refs[3:8]
    part_refs = lanes_of(*refs[8:11])
    ds_ref, p_ref = refs[11:13]
    k_all, v_all, s_all, w_all, p_all, stat = refs[13:]
    _, lanes, depth = qr_ref.shape
    kv_heads = kv_refs[0].shape[0] // 2
    rows = s_ref.shape[1]
    far = SPAN * rows
    scale = depth ** -0.5
    rate = scale * math.log2(math.e)
    group = lanes // rows
    chunks = lanes // WIDTH
    steps = [(c, n) for c in range(kv_heads) for n in range(chunks)]
    fold = lambda x: x.reshape(TILE // 8, 8, WIDTH)
    region = pl.when(me_ref[0] >= 0)
    tiles = [slice(r, r + TILE) for r in range(0, far, TILE)]

    def inside(r, n):
        local = lax.broadcasted_iota(jnp.int32, (TILE, WIDTH), 0) + r
        token = lax.broadcasted_iota(jnp.int32, (TILE, WIDTH), 1) // group + n * (WIDTH // group)
        return local <= token

    def gather(c):
        for o in range(SPAN):
            k_all[c % 2, o * rows : (o + 1) * rows, :] = kv_refs[o][c]
            v_all[c % 2, o * rows : (o + 1) * rows, :] = kv_refs[o][kv_heads + c]

    def score(t):
        c, n = steps[t]
        slot, cols = t % 2, slice(n * WIDTH, (n + 1) * WIDTH)
        s = dot(k_all[c % 2], qr_ref[first + c, cols, :], NT)
        top = jnp.full((8, WIDTH), HIDDEN, F32)
        for at in tiles:
            s_tile = s[at]
            if at.start < rows:
                s_tile = jnp.where(inside(at.start, n), s_ref[first + c, at, cols], s_tile)
            s_tile = s_tile + bias_ref[at, cols]
            s_all[slot, at, :] = s_tile
            top = jnp.maximum(top, jnp.max(fold(s_tile), axis=0))
        stat[slot, 0] = jnp.broadcast_to(jnp.max(top, axis=0, keepdims=True), (8, WIDTH))

    def weigh(t):
        c, n = steps[t]
        slot, cols = t % 2, slice(n * WIDTH, (n + 1) * WIDTH)
        w = dot(v_all[c % 2], gr_ref[first + c, cols, :], NT)
        for at in tiles:
            w_tile = w[at]
            if at.start < rows:
                w_tile = jnp.where(inside(at.start, n), w_ref[first + c, at, cols], w_tile)
            w_all[slot, at, :] = w_tile

    def spread(t):
        slot = t % 2
        top = stat[slot, 0, 0:1, :]
        total = jnp.zeros((8, WIDTH), F32)
        delta = jnp.zeros((8, WIDTH), F32)
        for at in tiles:
            e = jnp.exp2((s_all[slot, at, :] - top) * rate)
            s_all[slot, at, :] = e
            total = total + jnp.sum(fold(e), axis=0)
            delta = delta + jnp.sum(fold(e * w_all[slot, at, :]), axis=0)
        inverse = 1.0 / jnp.sum(total, axis=0, keepdims=True)
        delta = jnp.sum(delta, axis=0, keepdims=True) * inverse
        stat[slot, 1] = jnp.broadcast_to(inverse, (8, WIDTH))
        stat[slot, 2] = jnp.broadcast_to(delta, (8, WIDTH))

    def settle(t):
        c, n = steps[t]
        slot, cols = t % 2, slice(n * WIDTH, (n + 1) * WIDTH)
        inverse, delta = stat[slot, 1, 0:1, :], stat[slot, 2, 0:1, :]
        for at in tiles:
            prob = s_all[slot, at, :] * inverse
            dscore = ((prob * scale) * (w_all[slot, at, :] - delta)).astype(BF)
            prob = prob.astype(BF)
            if at.start < rows:
                here = inside(at.start, n)
                zero = jnp.zeros_like(prob)
                p_ref[c, at, cols] = jnp.where(here, prob, zero)
                ds_ref[c, far + at.start : far + at.stop, cols] = jnp.where(here, dscore, zero)
                prob = jnp.where(here, zero, prob)
                dscore = jnp.where(here, zero, dscore)
            p_all[c % 2, at, cols] = prob
            ds_ref[c, at, cols] = dscore

    def key_grad(c):
        dk = dot(ds_ref[c, :far, :], qr_ref[first + c], NN).astype(BF)
        for o in range(SPAN):
            part_refs[o][c] = dk[o * rows : (o + 1) * rows]

    def value_grad(c):
        dv = dot(p_all[c % 2], gr_ref[first + c], NN).astype(BF)
        for o in range(SPAN):
            part_refs[o][kv_heads + c] = dv[o * rows : (o + 1) * rows]

    @region
    def _():
        gather(0)

    @region
    def _():
        score(0)
        weigh(0)

    for t, (c, n) in enumerate(steps):
        following = t + 1 < len(steps)

        @region
        def _():
            spread(t)
            if n == chunks - 1 and following:
                gather(c + 1)
            if n == 0 and c:
                key_grad(c - 1)
            if following and n < chunks - 1:
                score(t + 1)

        @region
        def _():
            settle(t)
            if n == 0 and c:
                value_grad(c - 1)
            if following:
                if n == chunks - 1:
                    score(t + 1)
                weigh(t + 1)

    @region
    def _():
        key_grad(kv_heads - 1)
        value_grad(kv_heads - 1)


def query_body(*refs):
    per = 6
    groups = [refs[per * i : per * (i + 1)] for i in range(CHUNKS)]
    qr_ref, gr_ref, dq_ref, own_ref, turned_ref = refs[per * CHUNKS :]
    kv_heads, lanes, depth = qr_ref.shape
    part = kv_heads // CHUNKS
    rows = dq_ref.shape[0]
    group = lanes // rows
    for c in range(kv_heads):
        *sent_refs, own_kv_ref, ds_ref, p_ref = groups[c // part]
        kv_refs = (*lanes_of(*sent_refs), own_kv_ref)
        at = c % part
        own_ref[c] = dot(ds_ref[at, SPAN * rows :, :], qr_ref[c], NN)
        own_ref[kv_heads + c] = dot(p_ref[at], gr_ref[c], NN)
        for o in range(SPAN + 1):
            turned_ref[:, o * rows : (o + 1) * rows] = kv_refs[o][at].astype(F32).T.astype(BF)
        dq = dot(turned_ref[...], ds_ref[at], NN).T
        dq_ref[:, c * group : (c + 1) * group, :] = dq.reshape(rows, group, depth).astype(BF)


def finish_body(own_ref, *refs):
    groups, (dk_ref, dv_ref, wide_ref) = [refs[3 * i : 3 * i + 3] for i in range(CHUNKS)], refs[3 * CHUNKS :]
    kv_heads, rows, _ = own_ref.shape
    kv_heads //= 2
    part = kv_heads // CHUNKS
    for half, out_ref in enumerate((dk_ref, dv_ref)):
        for c in range(kv_heads):
            total = own_ref[half * kv_heads + c]
            for ref in groups[c // part]:
                total = total + ref[half * part + c % part].astype(F32)
            wide_ref[half, pl.ds(c, rows, stride=kv_heads), :] = total
        out_ref[...] = wide_ref[half].astype(BF)


def per_device(queries, key_states, value_states, out_grad, bounds):
    rows, heads, depth = queries.shape
    kv_heads = key_states.shape[1]
    part = kv_heads // CHUNKS
    group = heads // kv_heads
    lanes = rows * group
    shape = jax.ShapeDtypeStruct
    my_index = lax.axis_index(AXES)
    odd = lax.rem(my_index, 2) == 1
    product = 2 * kv_heads * rows * lanes * depth
    block = shape((2 * part, rows, depth), BF)
    double = shape((4 * part, rows, depth), BF)
    zero = jnp.zeros(block.shape, BF)

    flat = shape((rows * kv_heads, depth), BF)
    owns = call(
        pack_body,
        (block,) * CHUNKS,
        (in_hbm(key_states.reshape(flat.shape)), in_hbm(value_states.reshape(flat.shape))),
        specs=[HBM] * 2,
        scratch=(pltpu.VMEM((2, *flat.shape), BF), pltpu.VMEM((2, *flat.shape), F32), pltpu.SemaphoreType.DMA((2,))),
    )
    sent = []
    for own in owns:
        sent.append(rotated_pair((own, own), 1))
    ready = call(
        prepare_body,
        (
            shape((kv_heads, lanes, depth), BF),
            shape((kv_heads, lanes, depth), BF),
            shape((SPAN * rows, lanes), F32),
            shape((kv_heads, rows, lanes), F32),
            shape((kv_heads, rows, lanes), F32),
        ),
        (my_index.reshape(1), in_hbm(queries), in_hbm(out_grad), bounds, *owns),
        specs=[SMEM, HBM, HBM] + [VMEM] * (1 + CHUNKS),
        scratch=(pltpu.VMEM(queries.shape, BF), pltpu.VMEM(queries.shape, BF), pltpu.SemaphoreType.DMA((2,))),
        flops=2 * product,
    )
    qr, gr = ready[:2]
    blocks, scores, backs, rests = [], [], [], []
    parts = back = None
    for i in range(CHUNKS):
        (far, near), ready = lax.optimization_barrier((sent[i], ready))
        pair = swapped(jnp.concatenate([near, jnp.where(odd, far, owns[i])]))
        if back is not None:
            pair, back = lax.optimization_barrier((pair, back))
            backs.append(rotated_pair(back, -1))
        *parts, dscore, prob = call(
            functools.partial(main_body, i * part),
            (block, block, double)
            + (
                shape((part, (SPAN + 1) * rows, lanes), BF),
                shape((part, rows, lanes), BF),
            ),
            (my_index.reshape(1), far, near, pair, *ready),
            specs=[SMEM] + [VMEM] * 8,
            scratch=(
                pltpu.VMEM((2, SPAN * rows, depth), BF),
                pltpu.VMEM((2, SPAN * rows, depth), BF),
                pltpu.VMEM((2, SPAN * rows, WIDTH), F32),
                pltpu.VMEM((2, SPAN * rows, WIDTH), F32),
                pltpu.VMEM((2, SPAN * rows, lanes), BF),
                pltpu.VMEM((2, 3, 8, WIDTH), F32),
            ),
            flops=16 * product // CHUNKS,
            mib=18,
        )
        blocks.append((far, near, pair, owns[i]))
        scores.append((dscore, prob))
        if i + 1 < CHUNKS:
            sent[i + 1], parts = lax.optimization_barrier((sent[i + 1], parts))
        g_far, g_near, g_pair = parts
        back_x, back_y = jnp.split(swapped(g_pair), 2)
        back = (
            (g_far.astype(F32) + jnp.where(odd, back_y, zero).astype(F32)).astype(BF),
            (g_near.astype(F32) + back_x.astype(F32)).astype(BF),
        )
        rests.append(jnp.where(odd, zero, back_y))
    back, scores[-1] = lax.optimization_barrier((back, scores[-1]))
    backs.append(rotated_pair(back, -1))
    inputs = []
    for block_refs, score in zip(blocks, scores):
        inputs += [*block_refs, *score]
    dq, own_sum = call(
        query_body,
        (shape((rows, heads, depth), BF), shape((2 * kv_heads, rows, depth), F32)),
        (*inputs, qr, gr),
        scratch=(pltpu.VMEM((depth, (SPAN + 1) * rows), BF),),
        flops=7 * product,
    )
    inputs = []
    for rest, got in zip(rests, backs):
        inputs += [rest, *got]
    dk, dv = call(finish_body, (flat, flat), (own_sum, *inputs), scratch=(pltpu.VMEM((2, *flat.shape), F32),))
    return dq, dk.reshape(key_states.shape), dv.reshape(value_states.shape)


def solution(mesh):
    rows = P(AXES, None, None)

    return jax.shard_map(
        per_device,
        mesh=mesh,
        in_specs=(rows, rows, rows, rows, P(None, AXES)),
        out_specs=(rows, rows, rows),
        check_vma=False,
    )
```

```python
import functools
import math

import jax
import jax.numpy as jnp
from jax import lax
from jax.experimental import pallas as pl
from jax.experimental.pallas import tpu as pltpu
from jax.sharding import PartitionSpec as P


AXES = ("outer", "inner")
SPAN = 4
HIDDEN = -1e30
VMEM = pl.BlockSpec(memory_space=pltpu.VMEM)
SMEM = pl.BlockSpec(memory_space=pltpu.SMEM)
HBM = pl.BlockSpec(memory_space=pltpu.HBM)
NT = (((1,), (1,)), ((), ()))
NN = (((1,), (0,)), ((), ()))
BF = jnp.bfloat16
F32 = jnp.float32
TILE = 64
WIDTH = 512
CHUNKS = 2


def rotated(shard, by):
    peers = lax.axis_size(AXES)
    return lax.ppermute(shard, AXES, [(i, (i + by) % peers) for i in range(peers)])


def rotated_pair(shards, way):
    far = rotated(shards[0], way * SPAN)
    near = rotated(shards[1], way * SPAN // 2)
    return far, near


def swapped(shard):
    peers = lax.axis_size(AXES)
    return lax.ppermute(shard, AXES, [(i, i ^ 1) for i in range(peers)])


def dot(a, b, dims):
    return lax.dot_general(a, b, dims, preferred_element_type=F32)


def in_hbm(x):
    return pltpu.with_memory_space_constraint(x, pltpu.HBM)


def call(body, outs, args, specs=None, scratch=(), flops=0, mib=16):
    return pl.pallas_call(
        body,
        out_shape=outs,
        in_specs=specs or [VMEM] * len(args),
        out_specs=jax.tree.map(lambda _: VMEM, outs),
        scratch_shapes=list(scratch),
        compiler_params=pltpu.CompilerParams(vmem_limit_bytes=mib << 20),
        cost_estimate=pl.CostEstimate(flops=flops, bytes_accessed=1 << 20, transcendentals=0),
    )(*args)


def fetch(sources, targets, sems):
    copies = [pltpu.make_async_copy(a, b, sems.at[i]) for i, (a, b) in enumerate(zip(sources, targets))]
    for copy in copies:
        copy.start()
    return copies


def pack_body(k_hbm, v_hbm, *refs):
    kv_refs, (raw_ref, wide_ref, sems) = refs[:-3], refs[-3:]
    part, rows, _ = kv_refs[0].shape
    part //= 2
    heads = part * CHUNKS
    copies = fetch((k_hbm, v_hbm), (raw_ref.at[0], raw_ref.at[1]), sems)
    for half in range(2):
        copies[half].wait()
        wide_ref[half] = raw_ref[half].astype(F32)
        for c in range(heads):
            kv_refs[c // part][half * part + c % part] = wide_ref[half, pl.ds(c, rows, stride=heads), :].astype(BF)


def prepare_body(me_ref, q_hbm, g_hbm, bounds_hbm, *refs):
    kv_refs, outs = refs[:CHUNKS], refs[CHUNKS:]
    qr_ref, gr_ref, bias_ref, outside_ref, sides_ref, s_ref, w_ref, q_ref, g_ref, bounds_ref, inside_ref, sems = outs
    first, *copies = fetch((bounds_hbm, q_hbm, g_hbm), (bounds_ref, q_ref, g_ref), sems)
    first.wait()
    rows, heads, depth = q_ref.shape
    kv_heads = qr_ref.shape[0]
    part = kv_heads // CHUNKS
    group = heads // kv_heads
    lanes = rows * group
    local = lax.broadcasted_iota(jnp.int32, (rows, rows), 0)
    token = lax.broadcasted_iota(jnp.int32, (rows, rows), 1)
    wide_token = lax.broadcasted_iota(jnp.int32, (rows, lanes), 0)
    wide_lane = lax.broadcasted_iota(jnp.int32, (rows, lanes), 1)
    widen = (wide_lane // group == wide_token).astype(BF)
    me = me_ref[0]
    odd = lax.rem(me, 2)
    start = bounds_ref[0:1, :] - me * rows
    low = bounds_ref[1:2, :] - me * rows
    high = bounds_ref[2:3, :] - me * rows
    x_offset = 1 + 2 * odd

    key_any = local >= 0

    def hidden(offset, also):
        key = local - offset * rows
        seen = (key >= start) & ((key < low) | (key >= high)) & also
        return dot(jnp.where(seen, 0.0, HIDDEN).astype(BF), widen, NN)

    inside = local <= token
    inside_ref[0] = hidden(0, inside)
    for at, offset in enumerate((SPAN, 2, x_offset, SPAN - x_offset)):
        bias_ref[at * rows : (at + 1) * rows, :] = hidden(offset, ~inside if at == 0 else key_any)
    wide = dot(inside.astype(F32).astype(BF), widen, NN)
    inside_ref[1] = wide
    sides_ref[0] = wide.astype(BF)
    wide = 1.0 - wide
    outside_ref[...] = wide
    sides_ref[1] = wide.astype(BF)
    for copy in copies:
        copy.wait()
    for c in range(kv_heads):
        own = slice(c * group, (c + 1) * group)
        qr_ref[c] = q_ref[:, own, :].astype(F32).reshape(lanes, depth).astype(BF)
        gr_ref[c] = g_ref[:, own, :].astype(F32).reshape(lanes, depth).astype(BF)
        s_ref[c] = dot(kv_refs[c // part][c % part], qr_ref[c], NT) + inside_ref[0]
        w_ref[c] = dot(kv_refs[c // part][part + c % part], gr_ref[c], NT) * inside_ref[1]


def lanes_of(far_ref, near_ref, pair_ref):
    half = pair_ref.shape[0] // 2
    return far_ref, near_ref, pair_ref.at[:half], pair_ref.at[half:]


def key_value_grads(ds_ref, p_ref, q_ref, g_ref, out_refs, c):
    part, rows, _ = out_refs[0].shape
    dk = dot(ds_ref[...], q_ref[...], NN).astype(BF)
    dv = dot(p_ref[...], g_ref[...], NN).astype(BF)
    for i, ref in enumerate(out_refs):
        ref[c] = dk[i * rows : (i + 1) * rows]
        ref[part // 2 + c] = dv[i * rows : (i + 1) * rows]


def main_body(first, *refs):
    kv_refs = lanes_of(*refs[:3])
    qr_ref, gr_ref, bias_ref, outside_ref, sides_ref, s_ref, w_ref = refs[3:10]
    pair_ref, ds_ref, p_ref, rest_ref, k_all, v_all, p_all = refs[10:]
    _, lanes, depth = qr_ref.shape
    kv_heads = kv_refs[0].shape[0] // 2
    rows = s_ref.shape[1]
    far = SPAN * rows
    scale = depth ** -0.5
    rate = scale * math.log2(math.e)
    chunks = lanes // WIDTH
    fold = lambda x: x.reshape(TILE // 8, 8, WIDTH)
    tiles = [slice(r, r + TILE) for r in range(0, far, TILE)]

    def chunk(c, n):
        cols = slice(n * WIDTH, (n + 1) * WIDTH)
        s = dot(k_all[...], qr_ref[first + c, cols, :], NT)
        w = dot(v_all[...], gr_ref[first + c, cols, :], NT)
        top = jnp.full((8, WIDTH), HIDDEN, F32)
        scores, weighs, raws = [], [], []
        for at in tiles:
            s_tile = s[at] + bias_ref[at, cols]
            w_tile = w[at]
            if at.start < rows:
                s_tile = jnp.maximum(s_tile, s_ref[first + c, at, cols])
                w_tile = w_tile * outside_ref[at, cols] + w_ref[first + c, at, cols]
            scores.append(s_tile)
            weighs.append(w_tile)
            top = jnp.maximum(top, jnp.max(fold(s_tile), axis=0))
        top = jnp.max(top, axis=0, keepdims=True)
        total = jnp.zeros((8, WIDTH), F32)
        delta = jnp.zeros((8, WIDTH), F32)
        for s_tile, w_tile in zip(scores, weighs):
            e = jnp.exp2((s_tile - top) * rate)
            raws.append(e)
            total = total + jnp.sum(fold(e), axis=0)
            delta = delta + jnp.sum(fold(e * w_tile), axis=0)
        inverse = 1.0 / jnp.sum(total, axis=0, keepdims=True)
        delta = jnp.sum(delta, axis=0, keepdims=True) * inverse
        for at, e, w_tile in zip(tiles, raws, weighs):
            prob = e * inverse
            dscore = ((prob * scale) * (w_tile - delta)).astype(BF)
            prob = prob.astype(BF)
            if at.start < rows:
                inside, outside = sides_ref[0, at, cols], sides_ref[1, at, cols]
                p_ref[c, at, cols] = prob * inside
                ds_ref[c, far + at.start : far + at.stop, cols] = dscore * inside
                prob = prob * outside
                dscore = dscore * outside
            if at.start < 2 * rows:
                rest_ref[c, at, cols] = prob
            else:
                p_all[at.start - 2 * rows : at.stop - 2 * rows, cols] = prob
            ds_ref[c, at, cols] = dscore

    def head(c):
        for o in range(SPAN):
            k_all[o * rows : (o + 1) * rows, :] = kv_refs[o][c]
            v_all[o * rows : (o + 1) * rows, :] = kv_refs[o][kv_heads + c]
        for n in range(chunks):
            chunk(c, n)
        key_value_grads(ds_ref.at[c, 2 * rows : far], p_all, qr_ref.at[first + c], gr_ref.at[first + c], lanes_of(None, None, pair_ref)[2:], c)

    for c in range(kv_heads):
        head(c)


def rest_body(first, ds_ref, p_ref, qr_ref, gr_ref, far_ref, near_ref):
    part, count, _ = p_ref.shape
    for c in range(part):
        key_value_grads(ds_ref.at[c, :count], p_ref.at[c], qr_ref.at[first + c], gr_ref.at[first + c], (far_ref, near_ref), c)


def query_body(*refs):
    per = 6
    groups = [refs[per * i : per * (i + 1)] for i in range(CHUNKS)]
    qr_ref, gr_ref, dq_ref, own_ref, turned_ref = refs[per * CHUNKS :]
    kv_heads, lanes, depth = qr_ref.shape
    part = kv_heads // CHUNKS
    rows = dq_ref.shape[0]
    group = lanes // rows
    for c in range(kv_heads):
        *sent_refs, own_kv_ref, ds_ref, p_ref = groups[c // part]
        kv_refs = (*lanes_of(*sent_refs), own_kv_ref)
        at = c % part
        own_ref[c] = dot(ds_ref[at, SPAN * rows :, :], qr_ref[c], NN)
        own_ref[kv_heads + c] = dot(p_ref[at], gr_ref[c], NN)
        for o in range(SPAN + 1):
            turned_ref[:, o * rows : (o + 1) * rows] = kv_refs[o][at].astype(F32).T.astype(BF)
        dq = dot(turned_ref[...], ds_ref[at], NN).T
        dq_ref[:, c * group : (c + 1) * group, :] = dq.reshape(rows, group, depth).astype(BF)


def finish_body(own_ref, *refs):
    groups, (dk_ref, dv_ref, wide_ref) = [refs[3 * i : 3 * i + 3] for i in range(CHUNKS)], refs[3 * CHUNKS :]
    kv_heads, rows, _ = own_ref.shape
    kv_heads //= 2
    part = kv_heads // CHUNKS
    for half, out_ref in enumerate((dk_ref, dv_ref)):
        for c in range(kv_heads):
            total = own_ref[half * kv_heads + c]
            for ref in groups[c // part]:
                total = total + ref[half * part + c % part].astype(F32)
            wide_ref[half, pl.ds(c, rows, stride=kv_heads), :] = total
        out_ref[...] = wide_ref[half].astype(BF)


def per_device(queries, key_states, value_states, out_grad, bounds):
    rows, heads, depth = queries.shape
    kv_heads = key_states.shape[1]
    part = kv_heads // CHUNKS
    group = heads // kv_heads
    lanes = rows * group
    shape = jax.ShapeDtypeStruct
    my_index = lax.axis_index(AXES)
    odd = lax.rem(my_index, 2) == 1
    product = 2 * kv_heads * rows * lanes * depth
    block = shape((2 * part, rows, depth), BF)
    double = shape((4 * part, rows, depth), BF)
    zero = jnp.zeros(block.shape, BF)

    flat = shape((rows * kv_heads, depth), BF)
    owns = call(
        pack_body,
        (block,) * CHUNKS,
        (in_hbm(key_states.reshape(flat.shape)), in_hbm(value_states.reshape(flat.shape))),
        specs=[HBM] * 2,
        scratch=(pltpu.VMEM((2, *flat.shape), BF), pltpu.VMEM((2, *flat.shape), F32), pltpu.SemaphoreType.DMA((2,))),
    )
    sent = []
    for own in owns:
        sent.append(rotated_pair((own, own), 1))
    ready = call(
        prepare_body,
        (
            shape((kv_heads, lanes, depth), BF),
            shape((kv_heads, lanes, depth), BF),
            shape((SPAN * rows, lanes), F32),
            shape((rows, lanes), F32),
            shape((2, rows, lanes), BF),
            shape((kv_heads, rows, lanes), F32),
            shape((kv_heads, rows, lanes), F32),
        ),
        (my_index.reshape(1), in_hbm(queries), in_hbm(out_grad), in_hbm(bounds), *owns),
        specs=[SMEM, HBM, HBM, HBM] + [VMEM] * CHUNKS,
        scratch=(pltpu.VMEM(queries.shape, BF), pltpu.VMEM(queries.shape, BF), pltpu.VMEM(bounds.shape, jnp.int32), pltpu.VMEM((2, rows, lanes), F32), pltpu.SemaphoreType.DMA((3,))),
        flops=2 * product,
    )
    qr, gr = ready[:2]
    blocks, scores, backs, rests = [], [], [], []
    back = None
    for i in range(CHUNKS):
        (far, near), ready = lax.optimization_barrier((sent[i], ready))
        pair = swapped(jnp.concatenate([near, jnp.where(odd, far, owns[i])]))
        if back is not None:
            pair, back = lax.optimization_barrier((pair, back))
            backs.append(rotated_pair(back, -1))
        g_pair, dscore, prob, rest = call(
            functools.partial(main_body, i * part),
            (
                double,
                shape((part, (SPAN + 1) * rows, lanes), BF),
                shape((part, rows, lanes), BF),
                shape((part, 2 * rows, lanes), BF),
            ),
            (far, near, pair, *ready),
            scratch=(
                pltpu.VMEM((SPAN * rows, depth), BF),
                pltpu.VMEM((SPAN * rows, depth), BF),
                pltpu.VMEM((2 * rows, lanes), BF),
            ),
            flops=16 * product // CHUNKS,
            mib=20,
        )
        blocks.append((far, near, pair, owns[i]))
        scores.append((dscore, prob))
        if i + 1 < CHUNKS:
            sent[i + 1], g_pair = lax.optimization_barrier((sent[i + 1], g_pair))
        turned = swapped(g_pair)
        g_far, g_near = call(
            functools.partial(rest_body, i * part), (block, block), (dscore, rest, qr, gr), flops=2 * product // CHUNKS
        )
        back_x, back_y = jnp.split(turned, 2)
        back = (
            (g_far.astype(F32) + jnp.where(odd, back_y, zero).astype(F32)).astype(BF),
            (g_near.astype(F32) + back_x.astype(F32)).astype(BF),
        )
        rests.append(jnp.where(odd, zero, back_y))
    back, scores[-1] = lax.optimization_barrier((back, scores[-1]))
    backs.append(rotated_pair(back, -1))
    inputs = []
    for block_refs, score in zip(blocks, scores):
        inputs += [*block_refs, *score]
    dq, own_sum = call(
        query_body,
        (shape((rows, heads, depth), BF), shape((2 * kv_heads, rows, depth), F32)),
        (*inputs, qr, gr),
        scratch=(pltpu.VMEM((depth, (SPAN + 1) * rows), BF),),
        flops=7 * product,
    )
    inputs = []
    for rest, got in zip(rests, backs):
        inputs += [rest, *got]
    dk, dv = call(finish_body, (flat, flat), (own_sum, *inputs), scratch=(pltpu.VMEM((2, *flat.shape), F32),))
    return dq, dk.reshape(key_states.shape), dv.reshape(value_states.shape)


def solution(mesh):
    rows = P(AXES, None, None)

    return jax.shard_map(
        per_device,
        mesh=mesh,
        in_specs=(rows, rows, rows, rows, P(None, AXES)),
        out_specs=(rows, rows, rows),
        check_vma=False,
    )
```

```python
import functools
import math

import jax
import jax.numpy as jnp
from jax import lax
from jax.experimental import pallas as pl
from jax.experimental.pallas import tpu as pltpu
from jax.sharding import PartitionSpec as P


AXES = ("outer", "inner")
SPAN = 4
HIDDEN = -1e30
VMEM = pl.BlockSpec(memory_space=pltpu.VMEM)
SMEM = pl.BlockSpec(memory_space=pltpu.SMEM)
HBM = pl.BlockSpec(memory_space=pltpu.HBM)
NT = (((1,), (1,)), ((), ()))
NN = (((1,), (0,)), ((), ()))
BF = jnp.bfloat16
F32 = jnp.float32
TILE = 64
WIDTH = 512
CHUNKS = 2


def rotated(shard, by):
    peers = lax.axis_size(AXES)
    return lax.ppermute(shard, AXES, [(i, (i + by) % peers) for i in range(peers)])


def rotated_pair(shards, way):
    far = rotated(shards[0], way * SPAN)
    near = rotated(shards[1], way * SPAN // 2)
    return far, near


def swapped(shard):
    peers = lax.axis_size(AXES)
    return lax.ppermute(shard, AXES, [(i, i ^ 1) for i in range(peers)])


def dot(a, b, dims):
    return lax.dot_general(a, b, dims, preferred_element_type=F32)


def in_hbm(x):
    return pltpu.with_memory_space_constraint(x, pltpu.HBM)


def call(body, outs, args, specs=None, scratch=(), flops=0, mib=16):
    return pl.pallas_call(
        body,
        out_shape=outs,
        in_specs=specs or [VMEM] * len(args),
        out_specs=jax.tree.map(lambda _: VMEM, outs),
        scratch_shapes=list(scratch),
        compiler_params=pltpu.CompilerParams(vmem_limit_bytes=mib << 20),
        cost_estimate=pl.CostEstimate(flops=flops, bytes_accessed=1 << 20, transcendentals=0),
    )(*args)


def fetch(sources, targets, sems):
    copies = [pltpu.make_async_copy(a, b, sems.at[i]) for i, (a, b) in enumerate(zip(sources, targets))]
    for copy in copies:
        copy.start()
    return copies


def pack_body(k_hbm, v_hbm, *refs):
    kv_refs, (raw_ref, wide_ref, sems) = refs[:-3], refs[-3:]
    part, rows, _ = kv_refs[0].shape
    part //= 2
    heads = part * CHUNKS
    copies = fetch((k_hbm, v_hbm), (raw_ref.at[0], raw_ref.at[1]), sems)
    for half in range(2):
        copies[half].wait()
        wide_ref[half] = raw_ref[half].astype(F32)
        for c in range(heads):
            kv_refs[c // part][half * part + c % part] = wide_ref[half, pl.ds(c, rows, stride=heads), :].astype(BF)


def prepare_body(me_ref, q_hbm, g_hbm, bounds_ref, *refs):
    kv_refs, outs = refs[:CHUNKS], refs[CHUNKS:]
    qr_ref, gr_ref, bias_ref, outside_ref, sides_ref, s_ref, w_ref, q_ref, g_ref, inside_ref, sems = outs
    copies = fetch((q_hbm, g_hbm), (q_ref, g_ref), sems)
    rows, heads, depth = q_ref.shape
    kv_heads = qr_ref.shape[0]
    part = kv_heads // CHUNKS
    group = heads // kv_heads
    lanes = rows * group
    local = lax.broadcasted_iota(jnp.int32, (rows, rows), 0)
    token = lax.broadcasted_iota(jnp.int32, (rows, rows), 1)
    wide_token = lax.broadcasted_iota(jnp.int32, (rows, lanes), 0)
    wide_lane = lax.broadcasted_iota(jnp.int32, (rows, lanes), 1)
    widen = (wide_lane // group == wide_token).astype(BF)
    me = me_ref[0]
    odd = lax.rem(me, 2)
    start = bounds_ref[0:1, :] - me * rows
    low = bounds_ref[1:2, :] - me * rows
    high = bounds_ref[2:3, :] - me * rows
    x_offset = 1 + 2 * odd

    key_any = local >= 0

    def hidden(offset, also):
        key = local - offset * rows
        seen = (key >= start) & ((key < low) | (key >= high)) & also
        return dot(jnp.where(seen, 0.0, HIDDEN).astype(BF), widen, NN)

    inside = local <= token
    inside_ref[0] = hidden(0, inside)
    for at, offset in enumerate((SPAN, 2, x_offset, SPAN - x_offset)):
        bias_ref[at * rows : (at + 1) * rows, :] = hidden(offset, ~inside if at == 0 else key_any)
    wide = dot(inside.astype(F32).astype(BF), widen, NN)
    inside_ref[1] = wide
    sides_ref[0] = wide.astype(BF)
    wide = 1.0 - wide
    outside_ref[...] = wide
    sides_ref[1] = wide.astype(BF)
    for copy in copies:
        copy.wait()
    for c in range(kv_heads):
        own = slice(c * group, (c + 1) * group)
        qr_ref[c] = q_ref[:, own, :].astype(F32).reshape(lanes, depth).astype(BF)
        gr_ref[c] = g_ref[:, own, :].astype(F32).reshape(lanes, depth).astype(BF)
        s_ref[c] = dot(kv_refs[c // part][c % part], qr_ref[c], NT) + inside_ref[0]
        w_ref[c] = dot(kv_refs[c // part][part + c % part], gr_ref[c], NT) * inside_ref[1]


def lanes_of(far_ref, near_ref, pair_ref):
    half = pair_ref.shape[0] // 2
    return far_ref, near_ref, pair_ref.at[:half], pair_ref.at[half:]


def key_value_grads(ds_ref, p_ref, q_ref, g_ref, out_refs, c):
    part, rows, _ = out_refs[0].shape
    dk = dot(ds_ref[...], q_ref[...], NN).astype(BF)
    dv = dot(p_ref[...], g_ref[...], NN).astype(BF)
    for i, ref in enumerate(out_refs):
        ref[c] = dk[i * rows : (i + 1) * rows]
        ref[part // 2 + c] = dv[i * rows : (i + 1) * rows]


def main_body(first, *refs):
    kv_refs = lanes_of(*refs[:3])
    qr_ref, gr_ref, bias_ref, outside_ref, sides_ref, s_ref, w_ref = refs[3:10]
    pair_ref, ds_ref, p_ref, rest_ref, k_all, v_all, p_all = refs[10:]
    _, lanes, depth = qr_ref.shape
    kv_heads = kv_refs[0].shape[0] // 2
    rows = s_ref.shape[1]
    far = SPAN * rows
    scale = depth ** -0.5
    rate = scale * math.log2(math.e)
    chunks = lanes // WIDTH
    fold = lambda x: x.reshape(TILE // 8, 8, WIDTH)
    tiles = [slice(r, r + TILE) for r in range(0, far, TILE)]

    def chunk(c, n):
        cols = slice(n * WIDTH, (n + 1) * WIDTH)
        s = dot(k_all[...], qr_ref[first + c, cols, :], NT)
        w = dot(v_all[...], gr_ref[first + c, cols, :], NT)
        top = jnp.full((8, WIDTH), HIDDEN, F32)
        scores, weighs, raws = [], [], []
        for at in tiles:
            s_tile = s[at] + bias_ref[at, cols]
            w_tile = w[at]
            if at.start < rows:
                s_tile = jnp.maximum(s_tile, s_ref[first + c, at, cols])
                w_tile = w_tile * outside_ref[at, cols] + w_ref[first + c, at, cols]
            scores.append(s_tile)
            weighs.append(w_tile)
            top = jnp.maximum(top, jnp.max(fold(s_tile), axis=0))
        top = jnp.max(top, axis=0, keepdims=True)
        total = jnp.zeros((8, WIDTH), F32)
        delta = jnp.zeros((8, WIDTH), F32)
        for s_tile, w_tile in zip(scores, weighs):
            e = jnp.exp2((s_tile - top) * rate)
            raws.append(e)
            total = total + jnp.sum(fold(e), axis=0)
            delta = delta + jnp.sum(fold(e * w_tile), axis=0)
        inverse = 1.0 / jnp.sum(total, axis=0, keepdims=True)
        delta = jnp.sum(delta, axis=0, keepdims=True) * inverse
        for at, e, w_tile in zip(tiles, raws, weighs):
            prob = e * inverse
            dscore = ((prob * scale) * (w_tile - delta)).astype(BF)
            prob = prob.astype(BF)
            if at.start < rows:
                inside, outside = sides_ref[0, at, cols], sides_ref[1, at, cols]
                p_ref[c, at, cols] = prob * inside
                ds_ref[c, far + at.start : far + at.stop, cols] = dscore * inside
                prob = prob * outside
                dscore = dscore * outside
            if at.start < 2 * rows:
                rest_ref[c, at, cols] = prob
            else:
                p_all[at.start - 2 * rows : at.stop - 2 * rows, cols] = prob
            ds_ref[c, at, cols] = dscore

    def head(c):
        for o in range(SPAN):
            k_all[o * rows : (o + 1) * rows, :] = kv_refs[o][c]
            v_all[o * rows : (o + 1) * rows, :] = kv_refs[o][kv_heads + c]
        for n in range(chunks):
            chunk(c, n)
        key_value_grads(ds_ref.at[c, 2 * rows : far], p_all, qr_ref.at[first + c], gr_ref.at[first + c], lanes_of(None, None, pair_ref)[2:], c)

    for c in range(kv_heads):
        head(c)


def rest_body(first, ds_ref, p_ref, qr_ref, gr_ref, far_ref, near_ref):
    part, count, _ = p_ref.shape
    for c in range(part):
        key_value_grads(ds_ref.at[c, :count], p_ref.at[c], qr_ref.at[first + c], gr_ref.at[first + c], (far_ref, near_ref), c)


def query_body(*refs):
    per = 6
    groups = [refs[per * i : per * (i + 1)] for i in range(CHUNKS)]
    qr_ref, gr_ref, dq_ref, own_ref, turned_ref = refs[per * CHUNKS :]
    kv_heads, lanes, depth = qr_ref.shape
    part = kv_heads // CHUNKS
    rows = dq_ref.shape[0]
    group = lanes // rows
    for c in range(kv_heads):
        *sent_refs, own_kv_ref, ds_ref, p_ref = groups[c // part]
        kv_refs = (*lanes_of(*sent_refs), own_kv_ref)
        at = c % part
        own_ref[c] = dot(ds_ref[at, SPAN * rows :, :], qr_ref[c], NN)
        own_ref[kv_heads + c] = dot(p_ref[at], gr_ref[c], NN)
        for o in range(SPAN + 1):
            turned_ref[:, o * rows : (o + 1) * rows] = kv_refs[o][at].astype(F32).T.astype(BF)
        dq = dot(turned_ref[...], ds_ref[at], NN).T
        dq_ref[:, c * group : (c + 1) * group, :] = dq.reshape(rows, group, depth).astype(BF)


def finish_body(own_ref, *refs):
    groups, (dk_ref, dv_ref, wide_ref) = [refs[3 * i : 3 * i + 3] for i in range(CHUNKS)], refs[3 * CHUNKS :]
    kv_heads, rows, _ = own_ref.shape
    kv_heads //= 2
    part = kv_heads // CHUNKS
    for half, out_ref in enumerate((dk_ref, dv_ref)):
        for c in range(kv_heads):
            total = own_ref[half * kv_heads + c]
            for ref in groups[c // part]:
                total = total + ref[half * part + c % part].astype(F32)
            wide_ref[half, pl.ds(c, rows, stride=kv_heads), :] = total
        out_ref[...] = wide_ref[half].astype(BF)


def per_device(queries, key_states, value_states, out_grad, bounds):
    rows, heads, depth = queries.shape
    kv_heads = key_states.shape[1]
    part = kv_heads // CHUNKS
    group = heads // kv_heads
    lanes = rows * group
    shape = jax.ShapeDtypeStruct
    my_index = lax.axis_index(AXES)
    odd = lax.rem(my_index, 2) == 1
    product = 2 * kv_heads * rows * lanes * depth
    block = shape((2 * part, rows, depth), BF)
    double = shape((4 * part, rows, depth), BF)
    zero = jnp.zeros(block.shape, BF)

    flat = shape((rows * kv_heads, depth), BF)
    owns = call(
        pack_body,
        (block,) * CHUNKS,
        (in_hbm(key_states.reshape(flat.shape)), in_hbm(value_states.reshape(flat.shape))),
        specs=[HBM] * 2,
        scratch=(pltpu.VMEM((2, *flat.shape), BF), pltpu.VMEM((2, *flat.shape), F32), pltpu.SemaphoreType.DMA((2,))),
    )
    sent = []
    for own in owns:
        sent.append(rotated_pair((own, own), 1))
    ready = call(
        prepare_body,
        (
            shape((kv_heads, lanes, depth), BF),
            shape((kv_heads, lanes, depth), BF),
            shape((SPAN * rows, lanes), F32),
            shape((rows, lanes), F32),
            shape((2, rows, lanes), BF),
            shape((kv_heads, rows, lanes), F32),
            shape((kv_heads, rows, lanes), F32),
        ),
        (my_index.reshape(1), in_hbm(queries), in_hbm(out_grad), bounds, *owns),
        specs=[SMEM, HBM, HBM] + [VMEM] * (1 + CHUNKS),
        scratch=(pltpu.VMEM(queries.shape, BF), pltpu.VMEM(queries.shape, BF), pltpu.VMEM((2, rows, lanes), F32), pltpu.SemaphoreType.DMA((2,))),
        flops=2 * product,
    )
    qr, gr = ready[:2]
    blocks, scores, backs, rests = [], [], [], []
    back = None
    for i in range(CHUNKS):
        far, near = sent[i]
        pair = swapped(jnp.concatenate([near, jnp.where(odd, far, owns[i])]))
        if back is not None:
            pair, back = lax.optimization_barrier((pair, back))
            backs.append(rotated_pair(back, -1))
        g_pair, dscore, prob, rest = call(
            functools.partial(main_body, i * part),
            (
                double,
                shape((part, (SPAN + 1) * rows, lanes), BF),
                shape((part, rows, lanes), BF),
                shape((part, 2 * rows, lanes), BF),
            ),
            (far, near, pair, *ready),
            scratch=(
                pltpu.VMEM((SPAN * rows, depth), BF),
                pltpu.VMEM((SPAN * rows, depth), BF),
                pltpu.VMEM((2 * rows, lanes), BF),
            ),
            flops=16 * product // CHUNKS,
            mib=20,
        )
        blocks.append((far, near, pair, owns[i]))
        scores.append((dscore, prob))
        if i + 1 < CHUNKS:
            sent[i + 1], g_pair = lax.optimization_barrier((sent[i + 1], g_pair))
        turned = swapped(g_pair)
        g_far, g_near = call(
            functools.partial(rest_body, i * part), (block, block), (dscore, rest, qr, gr), flops=2 * product // CHUNKS
        )
        back_x, back_y = jnp.split(turned, 2)
        back = (
            (g_far.astype(F32) + jnp.where(odd, back_y, zero).astype(F32)).astype(BF),
            (g_near.astype(F32) + back_x.astype(F32)).astype(BF),
        )
        rests.append(jnp.where(odd, zero, back_y))
    back, scores[-1] = lax.optimization_barrier((back, scores[-1]))
    backs.append(rotated_pair(back, -1))
    inputs = []
    for block_refs, score in zip(blocks, scores):
        inputs += [*block_refs, *score]
    dq, own_sum = call(
        query_body,
        (shape((rows, heads, depth), BF), shape((2 * kv_heads, rows, depth), F32)),
        (*inputs, qr, gr),
        scratch=(pltpu.VMEM((depth, (SPAN + 1) * rows), BF),),
        flops=7 * product,
    )
    inputs = []
    for rest, got in zip(rests, backs):
        inputs += [rest, *got]
    dk, dv = call(finish_body, (flat, flat), (own_sum, *inputs), scratch=(pltpu.VMEM((2, *flat.shape), F32),))
    return dq, dk.reshape(key_states.shape), dv.reshape(value_states.shape)


def solution(mesh):
    rows = P(AXES, None, None)

    return jax.shard_map(
        per_device,
        mesh=mesh,
        in_specs=(rows, rows, rows, rows, P(None, AXES)),
        out_specs=(rows, rows, rows),
        check_vma=False,
    )
```
